32 devices in a mesh: dp: 8 (over z, core), col: 4 (over y, x).
Axes of the slice: x: 2, y: 2, z: 4, core: 2. Of those that a mesh axis runs over, the one named last changes fastest.
Arguments:
- features: bfloat16 [12288, 256], P(('dp', 'col')), may hold values from -6 to 6
- w_in: bfloat16 [256, 1024], replicated, may hold values from -0.375 to 0.375
- w_out: bfloat16 [1024, 64], replicated, may hold values from -0.1875 to 0.1875
- length_inv: float32 [64], replicated, may hold values from 0.2 to 0.6
- cg_vectors: bfloat16 [12288, 8], P(('dp', 'col')), may hold values from -6 to 6
- cotangent: bfloat16 [12288, 8], P(('dp', 'col')), may hold values from -6 to 6
Outputs:
- product: float32 [12288, 8], P(('dp', 'col'))
- grad_in: float32 [256, 1024], replicated
- grad_out: float32 [1024, 64], replicated
The draws below stay inside these ranges and needn't reach their ends.
All inputs are finite; a program needn't handle non-finite values.
Results may differ from the reference program's by a relative error of at most 0.03.
Values may be sent and summed in bfloat16 or wider, within the bound.
A program may use at most 64 MiB of HBM per device.

```python
import math
import jax
import jax.numpy as jnp
from jax import lax

FEAT = 256
HID = 1024
EMB = 64
RHS = 8
TOTAL = 12288


def block_levels(own_key, dims, split, smallest, top_value):
    loudness, own = 1.0, jax.random.fold_in(own_key, 6)
    for axis_at, blocks in split:
        steps = jnp.exp(jax.random.uniform(jax.random.fold_in(own, axis_at), (blocks,), jnp.float32, smallest / len(split), top_value / len(split)))
        loudness = loudness * jnp.repeat(steps, dims[axis_at] // blocks).reshape([-1 if axis == axis_at else 1 for axis in range(len(dims))])
    return loudness


def gaussian(rng, dims, width, most, split=(), dtype=jnp.bfloat16):
    entries = width * jax.random.normal(rng, dims, jnp.float32)
    if split:
        entries = entries * block_levels(rng, dims, split, -0.22, 0.18)
    return jnp.clip(entries, -most, most).astype(dtype)


def setup_inputs(seed: int = 0) -> dict:
    key_of = jax.random.split(jax.random.key(seed), 7)
    features = gaussian(key_of[0], (TOTAL, FEAT), 1.0, 6.0, ((0, 32),))
    w_in = gaussian(key_of[1], (FEAT, HID), FEAT ** -0.5, 0.375)
    w_out = gaussian(key_of[2], (HID, EMB), HID ** -0.5, 0.1875)
    length_inv = jnp.clip(jnp.exp(jax.random.uniform(key_of[3], (EMB,), jnp.float32, math.log(0.2), math.log(0.6))), 0.2, 0.6)
    cg_vectors = gaussian(key_of[4], (TOTAL, RHS), 1.0, 6.0, ((0, 32),))
    cotangent = gaussian(key_of[5], (TOTAL, RHS), 1.0, 6.0, ((0, 32),))
    return dict(features=features, w_in=w_in, w_out=w_out, length_inv=length_inv, cg_vectors=cg_vectors, cotangent=cotangent)


def reference(features, w_in, w_out, length_inv, cg_vectors, cotangent):
    f32 = jnp.float32
    pre = jnp.dot(features.astype(f32), w_in.astype(f32))
    hidden = jax.nn.silu(pre).astype(jnp.bfloat16)
    embed = jnp.dot(hidden.astype(f32), w_out.astype(f32)).astype(jnp.bfloat16)
    scaled = (embed.astype(f32) * length_inv).astype(jnp.bfloat16)
    zfull = scaled.astype(f32)
    sqfull = jnp.sum(zfull * zfull, axis=1)
    vfull = cg_vectors.astype(f32)
    mixed_col = jnp.concatenate([cg_vectors, cotangent], axis=1).astype(f32)
    mixed_row = jnp.concatenate([cotangent, cg_vectors], axis=1).astype(f32)
    block = math.gcd(TOTAL, 1024)
    count = TOTAL // block

    def one_block(args):
        zrow, sqrow, crow = args
        cross = jnp.dot(zrow, zfull.T)
        kern = jnp.exp(-0.5 * (sqrow[:, None] + sqfull[None, :] - 2.0 * cross)).astype(jnp.bfloat16)
        kernf = kern.astype(f32)
        prod = jnp.dot(kernf, vfull)
        pair = jnp.dot(crow, mixed_col.T)
        spair = (pair * kernf).astype(jnp.bfloat16).astype(f32)
        acc = jnp.dot(spair, zfull)
        rsum = jnp.sum(spair, axis=1)
        return prod, acc - rsum[:, None] * zrow

    prod, grad_scaled = lax.map(one_block, (zfull.reshape(count, block, EMB), sqfull.reshape(count, block), mixed_row.reshape(count, block, 2 * RHS)))
    product = prod.reshape(TOTAL, RHS)
    grad_scaled = grad_scaled.reshape(TOTAL, EMB)
    grad_embed = (grad_scaled * length_inv).astype(jnp.bfloat16).astype(f32)
    grad_out = jnp.dot(hidden.astype(f32).T, grad_embed)
    dhid = jnp.dot(grad_embed, w_out.astype(f32).T)
    sig = jax.nn.sigmoid(pre)
    grad_pre = (dhid * sig * (1.0 + pre * (1.0 - sig))).astype(jnp.bfloat16).astype(f32)
    grad_in = jnp.dot(features.astype(f32).T, grad_pre)
    return product, grad_in, grad_out
```

```python
import functools

import jax
import jax.numpy as jnp
from jax import lax
from jax.experimental import pallas as pl
from jax.experimental.pallas import tpu as pltpu
from jax.sharding import PartitionSpec as P

MESH = pl.DeviceIdType.MESH
f32 = jnp.float32
bf16 = jnp.bfloat16
LANES = 128
SUB = 16


def iota(shape, dim):
    return lax.broadcasted_iota(jnp.int32, shape, dim)


def dot(a, b, ca=1, cb=0):
    return lax.dot_general(a, b, (((ca,), (cb,)), ((), ())), preferred_element_type=f32)


def kernel(n_dp, n_col, tp, feat, w_in, w_out, linv, vec, cot, prod_o, gin_o, gout_o,
           hid, der, rows_s, cols_s, et, pt, sv, sz, acc, msg, part, gbuf, hbuf, rbuf, pbuf, fbuf,
           row_send, row_recv, col_send, col_recv, fwd_send, msg_send, msg_recv,
           core_send, core_recv, rs_send, rs_recv, ag_send, ag_recv):
    m, width = feat.shape[0], w_out.shape[1]
    rhs = vec.shape[1]
    hidden_units = w_in.shape[1]
    features_n = feat.shape[1]
    nz = n_dp // 2
    n2 = nz * n_col
    half = n2 * tp
    dp = lax.axis_index("dp")
    col = lax.axis_index("col")
    z = dp // 2
    core = dp - 2 * z
    mate = (2 * z + 1 - core, col)
    me2 = z * n_col + col

    def peer(k):
        q = lax.rem(me2 + k, n2)
        return q, (2 * (q // n_col) + core, lax.rem(q, n_col))

    barrier = pltpu.get_barrier_semaphore()
    pl.semaphore_signal(barrier, inc=1, device_id=mate, device_id_type=MESH)

    @pl.loop(1, n2)
    def _(k):
        pl.semaphore_signal(barrier, inc=1, device_id=peer(k)[1], device_id_type=MESH)

    pre = dot(feat[...], w_in[...])
    sig = 1.0 / (1.0 + jnp.exp(-pre))
    hid[...] = (pre * sig).astype(bf16)
    der[...] = sig * (1.0 + pre * (1.0 - sig))
    embed = dot(hid[...], w_out[...]).astype(bf16)
    scaled = (embed.astype(f32) * linv[...]).astype(bf16)
    zf = scaled.astype(f32)
    nh = -0.5 * jnp.sum(zf * zf, axis=1, keepdims=True)
    t0 = nh.astype(bf16).astype(f32)
    t1 = (nh - t0).astype(bf16).astype(f32)
    t2 = (nh - t0 - t1).astype(bf16).astype(f32)
    vat, cat, sat = width, width + rhs, width + 2 * rhs
    one = sat + 3

    def place(value, at):
        n = value.shape[1]
        sel = (iota((n, LANES), 1) == iota((n, LANES), 0) + at).astype(f32).astype(bf16)
        return dot(value, sel)

    lane = iota((m, LANES), 1)
    block = place(scaled, 0) + place(vec[...], vat) + place(cot[...], cat)
    block = jnp.where(lane == sat, t0, block)
    block = jnp.where(lane == sat + 1, t1, block)
    block = jnp.where(lane == sat + 2, t2, block)
    block = jnp.where((lane >= one) & (lane < one + 3), 1.0, block)
    block = block.astype(bf16)
    rows_s[col] = block
    cols_s[dp] = block

    pl.semaphore_wait(barrier, n2)

    def row_copy(to, slot):
        return pltpu.make_async_remote_copy(
            src_ref=rows_s.at[col], dst_ref=rows_s.at[slot], send_sem=row_send.at[to],
            recv_sem=row_recv.at[slot], device_id=(dp, to), device_id_type=MESH)

    def col_copy(to, slot):
        return pltpu.make_async_remote_copy(
            src_ref=cols_s.at[dp], dst_ref=cols_s.at[slot], send_sem=col_send.at[to],
            recv_sem=col_recv.at[slot], device_id=(to, col), device_id_type=MESH)

    def fwd_copy(slot):
        return pltpu.make_async_remote_copy(
            src_ref=cols_s.at[slot], dst_ref=cols_s.at[slot], send_sem=fwd_send.at[slot // 2],
            recv_sem=col_recv.at[slot], device_id=mate, device_id_type=MESH)

    def msg_copy(to, slot):
        return pltpu.make_async_remote_copy(
            src_ref=msg.at[to], dst_ref=part.at[slot], send_sem=msg_send.at[to],
            recv_sem=msg_recv.at[slot], device_id=(dp, to), device_id_type=MESH)

    col_copy(2 * z + 1 - core, dp).start()

    @pl.loop(1, nz)
    def _(k):
        col_copy(2 * lax.rem(z + k, nz) + core, dp).start()

    @pl.loop(1, n_col)
    def _(j):
        row_copy(lax.rem(col + j, n_col), col).start()

    acc[...] = jnp.zeros_like(acc)
    a, b = iota((2 * LANES, LANES), 0), iota((2 * LANES, LANES), 1)
    want = jnp.where(a < width, a, -1)
    want = jnp.where((a >= sat) & (a < one), a + 3, want)
    want = jnp.where((a >= one) & (a < one + 3), a - 3, want)
    low = a - LANES
    want = jnp.where((low >= vat) & (low < cat), low + rhs, want)
    want = jnp.where((low >= cat) & (low < sat), low - rhs, want)
    perm = (want == b).astype(f32).astype(bf16)
    keep_v = (lane >= vat) & (lane < cat)
    keep_z = (lane < width) | (lane == one)

    def prepare(zz):
        for side in range(2):
            blk = cols_s[2 * zz + side]
            ep = dot(perm, blk, 1, 1).astype(bf16)
            at = slice(side * m, (side + 1) * m)
            et[zz, :, at] = ep[:LANES]
            pt[zz, :, at] = ep[LANES:]
            wide = blk.astype(f32)
            sv[zz, at, :] = jnp.where(keep_v, wide, 0.0).astype(bf16)
            sz[zz, at, :] = jnp.where(keep_z, wide, 0.0).astype(bf16)

    def finish(chunk):
        total = acc[chunk]
        zrow = jnp.where(lane < width, rows_s[chunk].astype(f32), 0.0)
        return total - total[:, one:one + 1] * zrow

    @pl.loop(0, nz)
    def _(k):
        zz = lax.rem(z + k, nz)
        col_copy(dp, 2 * zz + 1 - core).wait_recv()
        prepare(zz)

        @pl.loop(0, n_col)
        def _(j):
            chunk = lax.rem(col + j + jnp.where(k == 0, 0, 1), n_col)

            @pl.when((k == 0) & (j > 0))
            def _():
                row_copy(col, chunk).wait_recv()

            lhs = rows_s[chunk]
            kern = jnp.exp(dot(lhs, et[zz]))
            pair = dot(lhs, pt[zz])
            kb = kern.astype(bf16)
            sp = (pair * kb.astype(f32)).astype(bf16)
            acc[chunk] += dot(kb, sv[zz]) + dot(sp, sz[zz])

            @pl.when((j == 0) & (k < nz - 1))
            def _():
                slot = 2 * lax.rem(z + k + 1, nz) + core
                col_copy(dp, slot).wait_recv()
                fwd_copy(slot).start()

            @pl.when((k == nz - 1) & (j < n_col - 1))
            def _():
                msg[chunk] = finish(chunk).astype(bf16)
                msg_copy(chunk, col).start()

    total = finish(col)
    for j in range(1, n_col):
        src = lax.rem(col + j, n_col)
        msg_copy(col, src).wait_recv()
        total = total + part[src].astype(f32)
    prod_o[...] = total[:, vat:cat]

    grad_embed = (total[:, :width] * linv[...]).astype(bf16)
    grad_pre = (dot(grad_embed, w_out[...], 1, 1) * der[...]).astype(bf16)
    gin = dot(feat[...], grad_pre, 0, 0).astype(bf16)
    gout = dot(grad_embed, hid[...], 0, 0).astype(bf16)
    lgroups = hidden_units // LANES
    rgroups_in = features_n // SUB
    rgroups = rgroups_in + width // SUB
    for rg in range(rgroups):
        for lg in range(lgroups):
            at = slice(lg * LANES, (lg + 1) * LANES)
            if rg < rgroups_in:
                tile = gin[rg * SUB:(rg + 1) * SUB, at]
            else:
                r = rg - rgroups_in
                tile = gout[r * SUB:(r + 1) * SUB, at]
            gbuf[rg * lgroups + lg] = tile
    used = rgroups * lgroups
    if used < 2 * half:
        gbuf[used:] = jnp.zeros((2 * half - used, SUB, LANES), bf16)

    give = pltpu.make_async_remote_copy(
        src_ref=gbuf.at[pl.ds((1 - core) * half, half)], dst_ref=hbuf, send_sem=core_send.at[0],
        recv_sem=core_recv.at[0], device_id=mate, device_id_type=MESH)
    give.start()
    give.wait_recv()
    rbuf[...] = (gbuf[pl.ds(core * half, half)].astype(f32) + hbuf[...].astype(f32)).astype(bf16)

    def rs_copy(q, device, slot):
        return pltpu.make_async_remote_copy(
            src_ref=rbuf.at[pl.ds(q * tp, tp)], dst_ref=pbuf.at[slot], send_sem=rs_send.at[q],
            recv_sem=rs_recv.at[slot], device_id=device, device_id_type=MESH)

    @pl.loop(1, n2)
    def _(k):
        q, device = peer(k)
        rs_copy(q, device, me2).start()

    def add(k, so_far):
        q, device = peer(k)
        rs_copy(q, device, q).wait_recv()
        return so_far + pbuf[q].astype(f32)

    mine = lax.fori_loop(1, n2, add, rbuf[pl.ds(me2 * tp, tp)].astype(f32))
    home = core * half
    fbuf[pl.ds(home + me2 * tp, tp)] = mine.astype(bf16)

    def ag_copy(q, device, slot):
        return pltpu.make_async_remote_copy(
            src_ref=fbuf.at[pl.ds(home + me2 * tp, tp)],
            dst_ref=fbuf.at[pl.ds(home + slot * tp, tp)], send_sem=ag_send.at[q],
            recv_sem=ag_recv.at[slot], device_id=device, device_id_type=MESH)

    @pl.loop(1, n2)
    def _(k):
        q, device = peer(k)
        ag_copy(q, device, me2).start()

    @pl.loop(1, n2)
    def _(k):
        q, device = peer(k)
        ag_copy(q, device, q).wait_recv()

    share = pltpu.make_async_remote_copy(
        src_ref=fbuf.at[pl.ds(home, half)], dst_ref=fbuf.at[pl.ds(home, half)],
        send_sem=core_send.at[1], recv_sem=core_recv.at[1], device_id=mate, device_id_type=MESH)
    share.start()

    col_copy(2 * z + 1 - core, dp).wait_send()
    give.wait_send()

    @pl.loop(1, nz)
    def _(k):
        zz = lax.rem(z + k, nz)
        col_copy(2 * zz + core, dp).wait_send()
        fwd_copy(2 * zz + core).wait_send()

    @pl.loop(1, n_col)
    def _(j):
        to = lax.rem(col + j, n_col)
        row_copy(to, col).wait_send()
        msg_copy(to, col).wait_send()

    @pl.loop(1, n2)
    def _(k):
        q, device = peer(k)
        rs_copy(q, device, me2).wait_send()
        ag_copy(q, device, me2).wait_send()

    pltpu.make_async_remote_copy(
        src_ref=fbuf.at[pl.ds(home, half)], dst_ref=fbuf.at[pl.ds((1 - core) * half, half)],
        send_sem=core_send.at[1], recv_sem=core_recv.at[1], device_id=mate,
        device_id_type=MESH).wait_recv()
    for rg in range(rgroups):
        for lg in range(lgroups):
            at = slice(lg * LANES, (lg + 1) * LANES)
            tile = fbuf[rg * lgroups + lg].astype(f32)
            if rg < rgroups_in:
                gin_o[rg * SUB:(rg + 1) * SUB, at] = tile
            else:
                r = rg - rgroups_in
                gout_o[r * SUB:(r + 1) * SUB, at] = tile
    share.wait_send()


def local(n_dp, n_col, features, w_in, w_out, length_inv, cg_vectors, cotangent):
    m, feat_n = features.shape
    hidden_units, width = w_out.shape
    rhs = cg_vectors.shape[1]
    nz, n2 = n_dp // 2, n_dp // 2 * n_col
    tiles = (feat_n + width) // SUB * (hidden_units // LANES)
    tp = -(-tiles // (2 * n2))
    half = n2 * tp
    dma = pltpu.SemaphoreType.DMA
    vm = pltpu.VMEM
    product, gin, gout = pl.pallas_call(
        functools.partial(kernel, n_dp, n_col, tp),
        out_shape=(
            jax.ShapeDtypeStruct((m, rhs), f32),
            jax.ShapeDtypeStruct((feat_n, hidden_units), f32),
            jax.ShapeDtypeStruct((width, hidden_units), f32),
        ),
        in_specs=[pl.BlockSpec(memory_space=vm)] * 6,
        out_specs=(pl.BlockSpec(memory_space=vm),) * 3,
        scratch_shapes=[
            vm((m, hidden_units), bf16),
            vm((m, hidden_units), f32),
            vm((n_col, m, LANES), bf16),
            vm((n_dp, m, LANES), bf16),
            vm((nz, LANES, 2 * m), bf16),
            vm((nz, LANES, 2 * m), bf16),
            vm((nz, 2 * m, LANES), bf16),
            vm((nz, 2 * m, LANES), bf16),
            vm((n_col, m, LANES), f32),
            vm((n_col, m, LANES), bf16),
            vm((n_col, m, LANES), bf16),
            vm((2 * half, SUB, LANES), bf16),
            vm((half, SUB, LANES), bf16),
            vm((half, SUB, LANES), bf16),
            vm((n2, tp, SUB, LANES), bf16),
            vm((2 * half, SUB, LANES), bf16),
            dma((n_col,)), dma((n_col,)),
            dma((n_dp,)), dma((n_dp,)), dma((nz,)),
            dma((n_col,)), dma((n_col,)),
            dma((2,)), dma((2,)),
            dma((n2,)), dma((n2,)), dma((n2,)), dma((n2,)),
        ],
        compiler_params=pltpu.CompilerParams(
            collective_id=0, has_side_effects=True, vmem_limit_bytes=48 << 20
        ),
    )(features, w_in, w_out, length_inv.reshape(1, width), cg_vectors, cotangent)
    return product, gin, gout.T


def solution(mesh):
    placed = (P(("dp", "col"), None), P(), P(), P(), P(("dp", "col"), None), P(("dp", "col"), None))
    return jax.shard_map(
        functools.partial(local, mesh.shape["dp"], mesh.shape["col"]),
        mesh=mesh,
        in_specs=placed,
        out_specs=(P(("dp", "col"), None), P(), P()),
        check_vma=False,
    )
```

```python
import functools

import jax
import jax.numpy as jnp
from jax import lax
from jax.experimental import pallas as pl
from jax.experimental.pallas import tpu as pltpu
from jax.sharding import PartitionSpec as P

MESH = pl.DeviceIdType.MESH
f32 = jnp.float32
bf16 = jnp.bfloat16
LANES = 128
SUB = 16


def iota(shape, dim):
    return lax.broadcasted_iota(jnp.int32, shape, dim)


def dot(a, b, ca=1, cb=0):
    return lax.dot_general(a, b, (((ca,), (cb,)), ((), ())), preferred_element_type=f32)


def kernel(n_dp, n_col, tp, feat_h, w_in_h, w_out_h, linv_h, vec_h, cot_h, prod_o, gin_o, gout_o,
           feat, w_in, w_out, linv, vec, cot, hid, der, feat_t, rows_t, rows_s, cols_t, et, pt, sv, sz,
           acc, msg, part, gbuf, hbuf, rbuf, xbuf, yout, yin, fbuf,
           in_sem, row_send, row_recv, line_send, col_recv, fwd_send, msg_send, msg_recv,
           core_send, core_recv, xy_send, xy_recv, z_send, z_recv,
           agz_send, agx_send, ag_recv, mate_send, mate_recv):
    loads = [
        pltpu.make_async_copy(src, dst, in_sem.at[i])
        for i, (src, dst) in enumerate([
            (feat_h, feat), (w_in_h, w_in), (w_out_h, w_out), (linv_h, linv), (vec_h, vec), (cot_h, cot)])
    ]
    for load in loads:
        load.start()
    m, width = feat.shape[0], w_out.shape[0]
    rhs = vec.shape[0]
    hidden_units = w_in.shape[1]
    features_n = feat.shape[1]
    nz = n_dp // 2
    n2 = nz * n_col
    half = n2 * tp
    dp = lax.axis_index("dp")
    col = lax.axis_index("col")
    z = dp // 2
    core = dp - 2 * z
    mate = (2 * z + 1 - core, col)
    zc = n_col * tp
    home = core * half

    def z_at(s):
        return lax.rem(z + s, nz)

    def col_at(j):
        return lax.rem(col + j, n_col)

    barrier = pltpu.get_barrier_semaphore()
    pl.semaphore_signal(barrier, inc=1, device_id=mate, device_id_type=MESH)

    @pl.loop(1, nz)
    def _(s):
        pl.semaphore_signal(barrier, inc=1, device_id=(2 * z_at(s) + core, col), device_id_type=MESH)

    @pl.loop(1, n_col)
    def _(j):
        pl.semaphore_signal(barrier, inc=1, device_id=(dp, col_at(j)), device_id_type=MESH)

    loads[0].wait()
    loads[1].wait()
    pre = dot(feat[...], w_in[...])
    sig = 1.0 / (1.0 + jnp.exp(-pre))
    hid[...] = (pre * sig).astype(bf16)
    der[...] = sig * (1.0 + pre * (1.0 - sig))
    for load in loads[2:]:
        load.wait()
    embed = dot(hid[...], w_out[...], 1, 1).astype(bf16)
    scaled = (embed.astype(f32) * linv[...]).astype(bf16)
    vat, cat, sat = width, width + rhs, width + 2 * rhs
    one = sat + 3
    pick = (iota((width, LANES), 1) == iota((width, LANES), 0)).astype(f32).astype(bf16)
    mine_t = jnp.concatenate(
        [dot(scaled, pick).T[:width], vec[...].astype(f32), cot[...].astype(f32)], axis=0).astype(bf16)
    rows_t[col] = mine_t
    cols_t[dp] = mine_t
    feat_t[...] = feat[...].T
    acc[...] = jnp.zeros_like(acc)

    pl.semaphore_wait(barrier, nz + n_col - 1)

    def row_copy(to, slot):
        return pltpu.make_async_remote_copy(
            src_ref=rows_t.at[col], dst_ref=rows_t.at[slot], send_sem=row_send.at[to],
            recv_sem=row_recv.at[slot], device_id=(dp, to), device_id_type=MESH)

    def line_copy(to, zi):
        slot = 2 * zi + core
        return pltpu.make_async_remote_copy(
            src_ref=cols_t.at[slot], dst_ref=cols_t.at[slot], send_sem=line_send.at[to],
            recv_sem=col_recv.at[slot], device_id=(2 * to + core, col), device_id_type=MESH)

    def fwd_copy(zi):
        slot = 2 * zi + core
        return pltpu.make_async_remote_copy(
            src_ref=cols_t.at[slot], dst_ref=cols_t.at[slot], send_sem=fwd_send.at[zi],
            recv_sem=col_recv.at[slot], device_id=mate, device_id_type=MESH)

    def from_mate(zi):
        slot = 2 * zi + 1 - core
        return pltpu.make_async_remote_copy(
            src_ref=cols_t.at[slot], dst_ref=cols_t.at[slot], send_sem=fwd_send.at[zi],
            recv_sem=col_recv.at[slot], device_id=mate, device_id_type=MESH)

    def msg_copy(to, slot):
        return pltpu.make_async_remote_copy(
            src_ref=msg.at[to], dst_ref=part.at[slot], send_sem=msg_send.at[to],
            recv_sem=msg_recv.at[slot], device_id=(dp, to), device_id_type=MESH)

    fwd_copy(z).start()

    both = jnp.minimum(z, nz - 1 - z)
    far = jnp.where(z < nz - 1 - z, 1, -1)

    def z_order(k):
        near = jnp.where(k % 2 == 1, (k + 1) // 2, -((k + 1) // 2))
        return z + jnp.where(k <= 2 * both, near, far * (k - both))

    @pl.loop(1, nz)
    def _(k):
        line_copy(z_order(k), z).start()

    @pl.loop(1, n_col)
    def _(j):
        row_copy(col_at(j), col).start()

    lane = iota((m, LANES), 1)
    sub_at = iota((LANES, m), 0)
    keep_v = (lane >= vat) & (lane < cat)
    keep_z = (lane < width) | (lane == one)

    def expand(block_t):
        wide = block_t.astype(f32)
        nh = -0.5 * jnp.sum(wide[:width] * wide[:width], axis=0, keepdims=True)
        t0 = nh.astype(bf16).astype(f32)
        t1 = (nh - t0).astype(bf16).astype(f32)
        t2 = (nh - t0 - t1).astype(bf16).astype(f32)
        rest = jnp.zeros((LANES - sat, m), f32)

        def tail(full, at_t, at_one):
            full = jnp.where(sub_at == at_t, t0, full)
            full = jnp.where(sub_at == at_t + 1, t1, full)
            full = jnp.where(sub_at == at_t + 2, t2, full)
            return jnp.where((sub_at >= at_one) & (sub_at < at_one + 3), 1.0, full)

        own = tail(jnp.concatenate([wide, rest], axis=0), sat, one)
        other = tail(jnp.concatenate([wide[:width], jnp.zeros((2 * rhs, m), f32), rest], axis=0), one, sat)
        swapped = jnp.concatenate(
            [jnp.zeros((width, m), f32), wide[cat:sat], wide[vat:cat], rest], axis=0)
        return own.T, other.astype(bf16), swapped.astype(bf16)

    def prepare(zz):
        for side in range(2):
            tall, other, swapped = expand(cols_t[2 * zz + side])
            at = slice(side * m, (side + 1) * m)
            et[zz, :, at] = other
            pt[zz, :, at] = swapped
            sv[zz, at, :] = jnp.where(keep_v, tall, 0.0).astype(bf16)
            sz[zz, at, :] = jnp.where(keep_z, tall, 0.0).astype(bf16)

    def tile(chunk, zz):
        lhs = rows_s[chunk]
        kern = jnp.exp(dot(lhs, et[zz]))
        pair = dot(lhs, pt[zz])
        kb = kern.astype(bf16)
        sp = (pair * kb.astype(f32)).astype(bf16)
        acc[chunk] += dot(kb, sv[zz]) + dot(sp, sz[zz])

    def finish(chunk):
        total = acc[chunk]
        zrow = jnp.where(lane < width, rows_s[chunk].astype(f32), 0.0)
        return (total - total[:, one:one + 1] * zrow).T[:sat]

    rows_s[col] = expand(mine_t)[0].astype(bf16)
    last = max(nz - 2, 1)

    @pl.loop(0, last)
    def _(k):
        zz = z_order(k)
        from_mate(zz).wait_recv()
        prepare(zz)

        @pl.loop(0, n_col)
        def _(j):
            chunk = col_at(j)

            @pl.when((k == 0) & (j > 0))
            def _():
                row_copy(col, chunk).wait_recv()
                rows_s[chunk] = expand(rows_t[chunk])[0].astype(bf16)

            tile(chunk, zz)
            t = k * n_col + j

            @pl.when((t % 2 == 1) & ((t + 1) // 2 < nz))
            def _():
                zi = z_order((t + 1) // 2)
                line_copy(zi, zi).wait_recv()
                fwd_copy(zi).start()

    @pl.loop(last, nz)
    def _(k):
        zz = z_order(k)
        from_mate(zz).wait_recv()
        prepare(zz)

    @pl.loop(0, n_col)
    def _(j):
        chunk = col_at(j + 1)

        @pl.loop(last, nz)
        def _(k):
            tile(chunk, z_order(k))

        @pl.when(j < n_col - 1)
        def _():
            msg[chunk] = finish(chunk).astype(bf16)
            msg_copy(chunk, col).start()

    total = finish(col)
    for j in range(1, n_col):
        src = lax.rem(col + j, n_col)
        msg_copy(col, src).wait_recv()
        total = total + part[src].astype(f32)
    prod_o[...] = total[vat:cat]

    square = (iota((width, width), 0) == iota((width, width), 1))
    scale = jnp.sum(jnp.where(square, linv[...], 0.0), axis=1, keepdims=True)
    grad_embed = (total[:width] * scale).astype(bf16)
    grad_pre = (dot(grad_embed, w_out[...], 0, 0) * der[...]).astype(bf16)
    gin = dot(feat_t[...], grad_pre).astype(bf16)
    gout = dot(grad_embed, hid[...]).astype(bf16)
    lgroups = hidden_units // LANES
    rgroups_in = features_n // SUB
    rgroups = rgroups_in + width // SUB
    for rg in range(rgroups):
        for lg in range(lgroups):
            at = slice(lg * LANES, (lg + 1) * LANES)
            if rg < rgroups_in:
                tile = gin[rg * SUB:(rg + 1) * SUB, at]
            else:
                r = rg - rgroups_in
                tile = gout[r * SUB:(r + 1) * SUB, at]
            gbuf[rg * lgroups + lg] = tile
    used = rgroups * lgroups
    if used < 2 * half:
        gbuf[used:] = jnp.zeros((2 * half - used, SUB, LANES), bf16)

    def swap_copy(zi):
        return pltpu.make_async_remote_copy(
            src_ref=gbuf.at[pl.ds((1 - core) * half + zi * zc, zc)], dst_ref=hbuf.at[pl.ds(zi * zc, zc)],
            send_sem=core_send.at[zi], recv_sem=core_recv.at[zi], device_id=mate, device_id_type=MESH)

    def xy_copy(zi, to, slot):
        return pltpu.make_async_remote_copy(
            src_ref=rbuf.at[pl.ds((zi * n_col + to) * tp, tp)], dst_ref=xbuf.at[zi, slot],
            send_sem=xy_send.at[zi, to], recv_sem=xy_recv.at[zi, slot],
            device_id=(dp, to), device_id_type=MESH)

    def z_copy(to, slot):
        return pltpu.make_async_remote_copy(
            src_ref=yout.at[to], dst_ref=yin.at[slot], send_sem=z_send.at[to], recv_sem=z_recv.at[slot],
            device_id=(2 * to + core, col), device_id_type=MESH)

    @pl.loop(0, nz)
    def _(s):
        swap_copy(z_at(s + 1)).start()

    @pl.loop(0, nz)
    def _(s):
        zi = z_at(s + 1)
        swap_copy(zi).wait_recv()
        here = pl.ds(zi * zc, zc)
        rbuf[here] = (gbuf[pl.ds(home + zi * zc, zc)].astype(f32) + hbuf[here].astype(f32)).astype(bf16)

        @pl.loop(1, n_col)
        def _(j):
            xy_copy(zi, col_at(j), col).start()

    def plane_sum(zi):
        def add(j, so_far):
            src = col_at(j)
            xy_copy(zi, src, src).wait_recv()
            return so_far + xbuf[zi, src].astype(f32)

        return lax.fori_loop(1, n_col, add, rbuf[pl.ds((zi * n_col + col) * tp, tp)].astype(f32))

    @pl.loop(0, nz - 1)
    def _(s):
        zi = z_at(s + 1)
        yout[zi] = plane_sum(zi).astype(bf16)
        z_copy(zi, z).start()

    def add_z(s, so_far):
        src = z_at(s)
        z_copy(src, src).wait_recv()
        return so_far + yin[src].astype(f32)

    mine = lax.fori_loop(1, nz, add_z, plane_sum(z))

    def piece(zi, ci):
        return fbuf.at[pl.ds(home + (zi * n_col + ci) * tp, tp)]

    def agz_copy(to, slot):
        return pltpu.make_async_remote_copy(
            src_ref=piece(slot, col), dst_ref=piece(slot, col), send_sem=agz_send.at[to],
            recv_sem=ag_recv.at[slot, col], device_id=(2 * to + core, col), device_id_type=MESH)

    def agx_copy(zi, to, slot):
        return pltpu.make_async_remote_copy(
            src_ref=piece(zi, slot), dst_ref=piece(zi, slot), send_sem=agx_send.at[zi, to],
            recv_sem=ag_recv.at[zi, slot], device_id=(dp, to), device_id_type=MESH)

    def mate_copy(zi, ci):
        return pltpu.make_async_remote_copy(
            src_ref=piece(zi, ci), dst_ref=piece(zi, ci), send_sem=mate_send.at[zi, ci],
            recv_sem=mate_recv.at[zi, ci], device_id=mate, device_id_type=MESH)

    fbuf[pl.ds(home + (z * n_col + col) * tp, tp)] = mine.astype(bf16)

    @pl.loop(1, nz)
    def _(s):
        agz_copy(z_at(s), z).start()

    @pl.loop(0, nz)
    def _(s):
        zi = z_at(s)

        @pl.when(s > 0)
        def _():
            agz_copy(zi, zi).wait_recv()

        @pl.loop(1, n_col)
        def _(j):
            agx_copy(zi, col_at(j), col).start()

        mate_copy(zi, col).start()

    @pl.loop(0, nz)
    def _(s):
        zi = z_at(s)

        @pl.loop(1, n_col)
        def _(j):
            src = col_at(j)
            agx_copy(zi, src, src).wait_recv()
            mate_copy(zi, src).start()

    fwd_copy(z).wait_send()

    @pl.loop(1, nz)
    def _(s):
        zz = z_at(s)
        line_copy(zz, z).wait_send()
        fwd_copy(zz).wait_send()
        z_copy(zz, z).wait_send()
        agz_copy(zz, z).wait_send()

    @pl.loop(1, n_col)
    def _(j):
        to = col_at(j)
        row_copy(to, col).wait_send()
        msg_copy(to, col).wait_send()

        @pl.loop(0, nz)
        def _(zi):
            xy_copy(zi, to, col).wait_send()
            agx_copy(zi, to, col).wait_send()

    @pl.loop(0, nz)
    def _(zi):
        swap_copy(zi).wait_send()

        @pl.loop(0, n_col)
        def _(ci):
            mate_copy(zi, ci).wait_send()

    @pl.loop(0, nz)
    def _(s):
        zi = z_at(s)

        @pl.loop(0, n_col)
        def _(j):
            ci = col_at(j)
            away = fbuf.at[pl.ds((1 - core) * half + (zi * n_col + ci) * tp, tp)]
            pltpu.make_async_remote_copy(
                src_ref=away, dst_ref=away, send_sem=mate_send.at[zi, ci],
                recv_sem=mate_recv.at[zi, ci], device_id=mate, device_id_type=MESH).wait_recv()

    for rg in range(rgroups):
        for lg in range(lgroups):
            at = slice(lg * LANES, (lg + 1) * LANES)
            tile_f = fbuf[rg * lgroups + lg].astype(f32)
            if rg < rgroups_in:
                gin_o[rg * SUB:(rg + 1) * SUB, at] = tile_f
            else:
                r = rg - rgroups_in
                gout_o[r * SUB:(r + 1) * SUB, at] = tile_f


def local(n_dp, n_col, features, w_in, w_out, length_inv, cg_vectors, cotangent):
    m, feat_n = features.shape
    hidden_units, width = w_out.shape
    rhs = cg_vectors.shape[1]
    nz, n2 = n_dp // 2, n_dp // 2 * n_col
    tiles = (feat_n + width) // SUB * (hidden_units // LANES)
    tp = -(-tiles // (2 * n2))
    half = n2 * tp
    dma = pltpu.SemaphoreType.DMA
    vm = pltpu.VMEM
    block = width + 2 * rhs
    product, gin, gout = pl.pallas_call(
        functools.partial(kernel, n_dp, n_col, tp),
        out_shape=(
            jax.ShapeDtypeStruct((rhs, m), f32),
            jax.ShapeDtypeStruct((feat_n, hidden_units), f32),
            jax.ShapeDtypeStruct((width, hidden_units), f32),
        ),
        in_specs=[pl.BlockSpec(memory_space=pltpu.HBM)] * 6,
        out_specs=(pl.BlockSpec(memory_space=vm),) * 3,
        scratch_shapes=[
            vm((m, feat_n), bf16),
            vm((feat_n, hidden_units), bf16),
            vm((width, hidden_units), bf16),
            vm((1, width), f32),
            vm((rhs, m), bf16),
            vm((rhs, m), bf16),
            vm((m, hidden_units), bf16),
            vm((m, hidden_units), f32),
            vm((feat_n, m), bf16),
            vm((n_col, block, m), bf16),
            vm((n_col, m, LANES), bf16),
            vm((n_dp, block, m), bf16),
            vm((nz, LANES, 2 * m), bf16),
            vm((nz, LANES, 2 * m), bf16),
            vm((nz, 2 * m, LANES), bf16),
            vm((nz, 2 * m, LANES), bf16),
            vm((n_col, m, LANES), f32),
            vm((n_col, block, m), bf16),
            vm((n_col, block, m), bf16),
            vm((2 * half, SUB, LANES), bf16),
            vm((half, SUB, LANES), bf16),
            vm((half, SUB, LANES), bf16),
            vm((nz, n_col, tp, SUB, LANES), bf16),
            vm((nz, tp, SUB, LANES), bf16),
            vm((nz, tp, SUB, LANES), bf16),
            vm((2 * half, SUB, LANES), bf16),
            dma((6,)), dma((n_col,)), dma((n_col,)),
            dma((nz,)), dma((n_dp,)), dma((nz,)),
            dma((n_col,)), dma((n_col,)),
            dma((nz,)), dma((nz,)),
            dma((nz, n_col)), dma((nz, n_col)),
            dma((nz,)), dma((nz,)),
            dma((nz,)), dma((nz, n_col)), dma((nz, n_col)),
            dma((nz, n_col)), dma((nz, n_col)),
        ],
        compiler_params=pltpu.CompilerParams(
            collective_id=0, has_side_effects=True, vmem_limit_bytes=60 << 20
        ),
    )(features, w_in, w_out.T, length_inv.reshape(1, width), cg_vectors.T, cotangent.T)
    return product.T, gin, gout.T


def solution(mesh):
    placed = (P(("dp", "col"), None), P(), P(), P(), P(("dp", "col"), None), P(("dp", "col"), None))
    return jax.shard_map(
        functools.partial(local, mesh.shape["dp"], mesh.shape["col"]),
        mesh=mesh,
        in_specs=placed,
        out_specs=(P(("dp", "col"), None), P(), P()),
        check_vma=False,
    )
```

```python
import functools

import jax
import jax.numpy as jnp
from jax import lax
from jax.experimental import pallas as pl
from jax.experimental.pallas import tpu as pltpu
from jax.sharding import PartitionSpec as P

MESH = pl.DeviceIdType.MESH
f32 = jnp.float32
bf16 = jnp.bfloat16
LANES = 128
SUB = 16


def iota(shape, dim):
    return lax.broadcasted_iota(jnp.int32, shape, dim)


def dot(a, b, ca=1, cb=0):
    return lax.dot_general(a, b, (((ca,), (cb,)), ((), ())), preferred_element_type=f32)


def kernel(n_dp, n_col, tp, feat_h, w_in_h, w_out_h, linv_h, vec_h, cot_h, prod_o, gin_o, gout_o,
           feat, w_in, w_out, linv, vec, cot, hid, der, feat_t, rows_t, rows_s, cols_t, et, pt, sv, sz,
           acc, msg, part, gbuf, hbuf, rbuf, xbuf, yout, yin, fbuf,
           in_sem, row_send, row_recv, line_send, col_recv, fwd_send, msg_send, msg_recv,
           core_send, core_recv, xy_send, xy_recv, z_send, z_recv,
           agz_send, agx_send, ag_recv, mate_send, mate_recv):
    loads = [
        pltpu.make_async_copy(src, dst, in_sem.at[i])
        for i, (src, dst) in enumerate([
            (feat_h, feat), (w_in_h, w_in), (w_out_h, w_out), (linv_h, linv), (vec_h, vec), (cot_h, cot)])
    ]
    for load in loads:
        load.start()
    m, width = feat.shape[0], w_out.shape[0]
    rhs = vec.shape[0]
    hidden_units = w_in.shape[1]
    features_n = feat.shape[1]
    nz = n_dp // 2
    n2 = nz * n_col
    half = n2 * tp
    dp = lax.axis_index("dp")
    col = lax.axis_index("col")
    z = dp // 2
    core = dp - 2 * z
    mate = (2 * z + 1 - core, col)
    zc = n_col * tp
    home = core * half

    def z_at(s):
        return lax.rem(z + s, nz)

    def col_at(j):
        return lax.rem(col + j, n_col)

    barrier = pltpu.get_barrier_semaphore()
    pl.semaphore_signal(barrier, inc=1, device_id=mate, device_id_type=MESH)

    @pl.loop(1, nz)
    def _(s):
        pl.semaphore_signal(barrier, inc=1, device_id=(2 * z_at(s) + core, col), device_id_type=MESH)

    @pl.loop(1, n_col)
    def _(j):
        pl.semaphore_signal(barrier, inc=1, device_id=(dp, col_at(j)), device_id_type=MESH)

    loads[0].wait()
    loads[1].wait()
    pre = dot(feat[...], w_in[...])
    sig = 1.0 / (1.0 + jnp.exp(-pre))
    hid[...] = (pre * sig).astype(bf16)
    der[...] = sig * (1.0 + pre * (1.0 - sig))
    for load in loads[2:]:
        load.wait()
    embed = dot(hid[...], w_out[...], 1, 1).astype(bf16)
    scaled = (embed.astype(f32) * linv[...]).astype(bf16)
    vat, cat, sat = width, width + rhs, width + 2 * rhs
    one = sat + 3
    pick = (iota((width, LANES), 1) == iota((width, LANES), 0)).astype(f32).astype(bf16)
    mine_t = jnp.concatenate(
        [dot(scaled, pick).T[:width], vec[...].astype(f32), cot[...].astype(f32)], axis=0).astype(bf16)
    rows_t[col] = mine_t
    cols_t[dp] = mine_t
    feat_t[...] = feat[...].T
    acc[...] = jnp.zeros_like(acc)

    pl.semaphore_wait(barrier, nz + n_col - 1)

    def row_copy(to, slot):
        return pltpu.make_async_remote_copy(
            src_ref=rows_t.at[col], dst_ref=rows_t.at[slot], send_sem=row_send.at[to],
            recv_sem=row_recv.at[slot], device_id=(dp, to), device_id_type=MESH)

    def line_copy(to, zi):
        slot = 2 * zi + core
        return pltpu.make_async_remote_copy(
            src_ref=cols_t.at[slot], dst_ref=cols_t.at[slot], send_sem=line_send.at[to],
            recv_sem=col_recv.at[slot], device_id=(2 * to + core, col), device_id_type=MESH)

    def fwd_copy(zi):
        slot = 2 * zi + core
        return pltpu.make_async_remote_copy(
            src_ref=cols_t.at[slot], dst_ref=cols_t.at[slot], send_sem=fwd_send.at[zi],
            recv_sem=col_recv.at[slot], device_id=mate, device_id_type=MESH)

    def from_mate(zi):
        slot = 2 * zi + 1 - core
        return pltpu.make_async_remote_copy(
            src_ref=cols_t.at[slot], dst_ref=cols_t.at[slot], send_sem=fwd_send.at[zi],
            recv_sem=col_recv.at[slot], device_id=mate, device_id_type=MESH)

    def msg_copy(to, slot):
        return pltpu.make_async_remote_copy(
            src_ref=msg.at[to], dst_ref=part.at[slot], send_sem=msg_send.at[to],
            recv_sem=msg_recv.at[slot], device_id=(dp, to), device_id_type=MESH)

    fwd_copy(z).start()

    both = jnp.minimum(z, nz - 1 - z)
    far = jnp.where(z < nz - 1 - z, 1, -1)

    def z_order(k):
        near = jnp.where(k % 2 == 1, (k + 1) // 2, -((k + 1) // 2))
        return z + jnp.where(k <= 2 * both, near, far * (k - both))

    @pl.loop(1, nz)
    def _(k):
        line_copy(z_order(k), z).start()

    @pl.loop(1, n_col)
    def _(j):
        row_copy(col_at(j), col).start()

    lane = iota((m, LANES), 1)
    sub_at = iota((LANES, m), 0)
    keep_v = (lane >= vat) & (lane < cat)
    keep_z = (lane < width) | (lane == one)

    def expand(block_t):
        wide = block_t.astype(f32)
        nh = -0.5 * jnp.sum(wide[:width] * wide[:width], axis=0, keepdims=True)
        t0 = nh.astype(bf16).astype(f32)
        t1 = (nh - t0).astype(bf16).astype(f32)
        t2 = (nh - t0 - t1).astype(bf16).astype(f32)
        rest = jnp.zeros((LANES - sat, m), f32)

        def tail(full, at_t, at_one):
            full = jnp.where(sub_at == at_t, t0, full)
            full = jnp.where(sub_at == at_t + 1, t1, full)
            full = jnp.where(sub_at == at_t + 2, t2, full)
            return jnp.where((sub_at >= at_one) & (sub_at < at_one + 3), 1.0, full)

        own = tail(jnp.concatenate([wide, rest], axis=0), sat, one)
        other = tail(jnp.concatenate([wide[:width], jnp.zeros((2 * rhs, m), f32), rest], axis=0), one, sat)
        swapped = jnp.concatenate(
            [jnp.zeros((width, m), f32), wide[cat:sat], wide[vat:cat], rest], axis=0)
        return own.T, other.astype(bf16), swapped.astype(bf16)

    def prepare(zz):
        for side in range(2):
            tall, other, swapped = expand(cols_t[2 * zz + side])
            at = slice(side * m, (side + 1) * m)
            et[zz, :, at] = other
            pt[zz, :, at] = swapped
            sv[zz, at, :] = jnp.where(keep_v, tall, 0.0).astype(bf16)
            sz[zz, at, :] = jnp.where(keep_z, tall, 0.0).astype(bf16)

    def tile(chunk, zz):
        lhs = rows_s[chunk]
        kern = jnp.exp(dot(lhs, et[zz]))
        pair = dot(lhs, pt[zz])
        kb = kern.astype(bf16)
        sp = (pair * kb.astype(f32)).astype(bf16)
        acc[chunk] += dot(kb, sv[zz]) + dot(sp, sz[zz])

    def finish(chunk):
        total = acc[chunk]
        zrow = jnp.where(lane < width, rows_s[chunk].astype(f32), 0.0)
        return (total - total[:, one:one + 1] * zrow).T[:sat]

    rows_s[col] = expand(mine_t)[0].astype(bf16)
    last = max(nz - 2, 1)

    @pl.loop(0, last)
    def _(k):
        zz = z_order(k)
        from_mate(zz).wait_recv()
        prepare(zz)

        @pl.loop(0, n_col)
        def _(j):
            chunk = col_at(j)

            @pl.when((k == 0) & (j > 0))
            def _():
                row_copy(col, chunk).wait_recv()
                rows_s[chunk] = expand(rows_t[chunk])[0].astype(bf16)

            tile(chunk, zz)
            t = k * n_col + j

            @pl.when((t % 2 == 1) & ((t + 1) // 2 < nz))
            def _():
                zi = z_order((t + 1) // 2)
                line_copy(zi, zi).wait_recv()
                fwd_copy(zi).start()

    @pl.loop(last, nz)
    def _(k):
        zz = z_order(k)
        from_mate(zz).wait_recv()
        prepare(zz)

    @pl.loop(0, n_col)
    def _(j):
        chunk = col_at(j + 1)

        @pl.loop(last, nz)
        def _(k):
            tile(chunk, z_order(k))

        @pl.when(j < n_col - 1)
        def _():
            msg[chunk] = finish(chunk).astype(bf16)
            msg_copy(chunk, col).start()

    total = finish(col)
    for j in range(1, n_col):
        src = lax.rem(col + j, n_col)
        msg_copy(col, src).wait_recv()
        total = total + part[src].astype(f32)
    prod_o[...] = total[vat:cat]

    square = (iota((width, width), 0) == iota((width, width), 1))
    scale = jnp.sum(jnp.where(square, linv[...], 0.0), axis=1, keepdims=True)
    grad_embed = (total[:width] * scale).astype(bf16)
    grad_pre = (dot(grad_embed, w_out[...], 0, 0) * der[...]).astype(bf16)
    gin = dot(feat_t[...], grad_pre).astype(bf16)
    gout = dot(grad_embed, hid[...]).astype(bf16)
    lgroups = hidden_units // LANES
    rgroups_in = features_n // SUB
    rgroups = rgroups_in + width // SUB
    for rg in range(rgroups):
        for lg in range(lgroups):
            at = slice(lg * LANES, (lg + 1) * LANES)
            if rg < rgroups_in:
                tile = gin[rg * SUB:(rg + 1) * SUB, at]
            else:
                r = rg - rgroups_in
                tile = gout[r * SUB:(r + 1) * SUB, at]
            gbuf[rg * lgroups + lg] = tile
    used = rgroups * lgroups
    if used < 2 * half:
        gbuf[used:] = jnp.zeros((2 * half - used, SUB, LANES), bf16)

    def swap_copy(zi):
        return pltpu.make_async_remote_copy(
            src_ref=gbuf.at[pl.ds((1 - core) * half + zi * zc, zc)], dst_ref=hbuf.at[pl.ds(zi * zc, zc)],
            send_sem=core_send.at[zi], recv_sem=core_recv.at[zi], device_id=mate, device_id_type=MESH)

    def xy_copy(zi, to, slot):
        return pltpu.make_async_remote_copy(
            src_ref=rbuf.at[pl.ds((zi * n_col + to) * tp, tp)], dst_ref=xbuf.at[zi, slot],
            send_sem=xy_send.at[zi, to], recv_sem=xy_recv.at[zi, slot],
            device_id=(dp, to), device_id_type=MESH)

    def z_copy(to, slot):
        return pltpu.make_async_remote_copy(
            src_ref=yout.at[to], dst_ref=yin.at[slot], send_sem=z_send.at[to], recv_sem=z_recv.at[slot],
            device_id=(2 * to + core, col), device_id_type=MESH)

    @pl.loop(0, nz)
    def _(s):
        swap_copy(z_at(s + 1)).start()

    @pl.loop(0, nz)
    def _(s):
        zi = z_at(s + 1)
        swap_copy(zi).wait_recv()
        here = pl.ds(zi * zc, zc)
        rbuf[here] = (gbuf[pl.ds(home + zi * zc, zc)].astype(f32) + hbuf[here].astype(f32)).astype(bf16)

        @pl.loop(1, n_col)
        def _(j):
            xy_copy(zi, col_at(j), col).start()

    def plane_sum(zi):
        def add(j, so_far):
            src = col_at(j)
            xy_copy(zi, src, src).wait_recv()
            return so_far + xbuf[zi, src].astype(f32)

        return lax.fori_loop(1, n_col, add, rbuf[pl.ds((zi * n_col + col) * tp, tp)].astype(f32))

    @pl.loop(0, nz - 1)
    def _(s):
        zi = z_at(s + 1)
        yout[zi] = plane_sum(zi).astype(bf16)
        z_copy(zi, z).start()

    def add_z(s, so_far):
        src = z_at(s)
        z_copy(src, src).wait_recv()
        return so_far + yin[src].astype(f32)

    mine = lax.fori_loop(1, nz, add_z, plane_sum(z))

    def piece(zi, ci):
        return fbuf.at[pl.ds(home + (zi * n_col + ci) * tp, tp)]

    def agz_copy(to, slot):
        return pltpu.make_async_remote_copy(
            src_ref=piece(slot, col), dst_ref=piece(slot, col), send_sem=agz_send.at[to],
            recv_sem=ag_recv.at[slot, col], device_id=(2 * to + core, col), device_id_type=MESH)

    def agx_copy(zi, to, slot):
        return pltpu.make_async_remote_copy(
            src_ref=piece(zi, slot), dst_ref=piece(zi, slot), send_sem=agx_send.at[zi, to],
            recv_sem=ag_recv.at[zi, slot], device_id=(dp, to), device_id_type=MESH)

    def mate_copy(zi, ci):
        return pltpu.make_async_remote_copy(
            src_ref=piece(zi, ci), dst_ref=piece(zi, ci), send_sem=mate_send.at[zi, ci],
            recv_sem=mate_recv.at[zi, ci], device_id=mate, device_id_type=MESH)

    fbuf[pl.ds(home + (z * n_col + col) * tp, tp)] = mine.astype(bf16)

    @pl.loop(1, nz)
    def _(s):
        agz_copy(z_at(s), z).start()

    @pl.loop(0, nz)
    def _(s):
        zi = z_at(s)

        @pl.when(s > 0)
        def _():
            agz_copy(zi, zi).wait_recv()

        @pl.loop(1, n_col)
        def _(j):
            agx_copy(zi, col_at(j), col).start()

        mate_copy(zi, col).start()

    @pl.loop(0, nz)
    def _(s):
        zi = z_at(s)

        @pl.loop(1, n_col)
        def _(j):
            src = col_at(j)
            agx_copy(zi, src, src).wait_recv()
            mate_copy(zi, src).start()

    fwd_copy(z).wait_send()

    @pl.loop(1, nz)
    def _(s):
        zz = z_at(s)
        line_copy(zz, z).wait_send()
        fwd_copy(zz).wait_send()
        z_copy(zz, z).wait_send()
        agz_copy(zz, z).wait_send()

    @pl.loop(1, n_col)
    def _(j):
        to = col_at(j)
        row_copy(to, col).wait_send()
        msg_copy(to, col).wait_send()

        @pl.loop(0, nz)
        def _(zi):
            xy_copy(zi, to, col).wait_send()
            agx_copy(zi, to, col).wait_send()

    @pl.loop(0, nz)
    def _(zi):
        swap_copy(zi).wait_send()

        @pl.loop(0, n_col)
        def _(ci):
            mate_copy(zi, ci).wait_send()

    @pl.loop(0, nz)
    def _(s):
        zi = z_at(s)

        @pl.loop(0, n_col)
        def _(j):
            ci = col_at(j)
            away = fbuf.at[pl.ds((1 - core) * half + (zi * n_col + ci) * tp, tp)]
            pltpu.make_async_remote_copy(
                src_ref=away, dst_ref=away, send_sem=mate_send.at[zi, ci],
                recv_sem=mate_recv.at[zi, ci], device_id=mate, device_id_type=MESH).wait_recv()

    for rg in range(rgroups):
        for lg in range(lgroups):
            at = slice(lg * LANES, (lg + 1) * LANES)
            tile_f = fbuf[rg * lgroups + lg]
            if rg < rgroups_in:
                gin_o[rg * SUB:(rg + 1) * SUB, at] = tile_f
            else:
                r = rg - rgroups_in
                gout_o[r * SUB:(r + 1) * SUB, at] = tile_f


def local(n_dp, n_col, features, w_in, w_out, length_inv, cg_vectors, cotangent):
    m, feat_n = features.shape
    hidden_units, width = w_out.shape
    rhs = cg_vectors.shape[1]
    nz, n2 = n_dp // 2, n_dp // 2 * n_col
    tiles = (feat_n + width) // SUB * (hidden_units // LANES)
    tp = -(-tiles // (2 * n2))
    half = n2 * tp
    dma = pltpu.SemaphoreType.DMA
    vm = pltpu.VMEM
    block = width + 2 * rhs
    product, gin, gout = pl.pallas_call(
        functools.partial(kernel, n_dp, n_col, tp),
        out_shape=(
            jax.ShapeDtypeStruct((rhs, m), f32),
            jax.ShapeDtypeStruct((feat_n, hidden_units), bf16),
            jax.ShapeDtypeStruct((width, hidden_units), bf16),
        ),
        in_specs=[pl.BlockSpec(memory_space=pltpu.HBM)] * 6,
        out_specs=(pl.BlockSpec(memory_space=vm),) * 3,
        scratch_shapes=[
            vm((m, feat_n), bf16),
            vm((feat_n, hidden_units), bf16),
            vm((width, hidden_units), bf16),
            vm((1, width), f32),
            vm((rhs, m), bf16),
            vm((rhs, m), bf16),
            vm((m, hidden_units), bf16),
            vm((m, hidden_units), f32),
            vm((feat_n, m), bf16),
            vm((n_col, block, m), bf16),
            vm((n_col, m, LANES), bf16),
            vm((n_dp, block, m), bf16),
            vm((nz, LANES, 2 * m), bf16),
            vm((nz, LANES, 2 * m), bf16),
            vm((nz, 2 * m, LANES), bf16),
            vm((nz, 2 * m, LANES), bf16),
            vm((n_col, m, LANES), f32),
            vm((n_col, block, m), bf16),
            vm((n_col, block, m), bf16),
            vm((2 * half, SUB, LANES), bf16),
            vm((half, SUB, LANES), bf16),
            vm((half, SUB, LANES), bf16),
            vm((nz, n_col, tp, SUB, LANES), bf16),
            vm((nz, tp, SUB, LANES), bf16),
            vm((nz, tp, SUB, LANES), bf16),
            vm((2 * half, SUB, LANES), bf16),
            dma((6,)), dma((n_col,)), dma((n_col,)),
            dma((nz,)), dma((n_dp,)), dma((nz,)),
            dma((n_col,)), dma((n_col,)),
            dma((nz,)), dma((nz,)),
            dma((nz, n_col)), dma((nz, n_col)),
            dma((nz,)), dma((nz,)),
            dma((nz,)), dma((nz, n_col)), dma((nz, n_col)),
            dma((nz, n_col)), dma((nz, n_col)),
        ],
        compiler_params=pltpu.CompilerParams(
            collective_id=0, has_side_effects=True, vmem_limit_bytes=60 << 20
        ),
    )(features, w_in, w_out.T, length_inv.reshape(1, width), cg_vectors.T, cotangent.T)
    return product.T, gin.astype(f32), gout.astype(f32).T


def solution(mesh):
    placed = (P(("dp", "col"), None), P(), P(), P(), P(("dp", "col"), None), P(("dp", "col"), None))
    return jax.shard_map(
        functools.partial(local, mesh.shape["dp"], mesh.shape["col"]),
        mesh=mesh,
        in_specs=placed,
        out_specs=(P(("dp", "col"), None), P(), P()),
        check_vma=False,
    )
```
